32 devices in a mesh: tm: 4 (over z), lat: 8 (over y, x, core).
Axes of the slice: x: 2, y: 2, z: 4, core: 2. Of those that a mesh axis runs over, the one named last changes fastest.
Arguments:
- frames: bfloat16 [256, 512, 1024], P('tm', 'lat'), may hold values from -6 to 6
- projection: bfloat16 [256, 512, 256], P(('tm', 'lat')), may hold values from -0.25 to 0.25
- degree_range: int32 [256, 2], replicated, may hold values from 0 to 256, as said below
- offsets: int32 [8], replicated, may hold values from 0 to 63
Outputs:
- coupling: bfloat16 [256, 2, 8, 256, 2, 256], P(('tm', 'lat'))
The draws below stay inside these ranges and needn't reach their ends.
Inputs may be any that keep to these rules, and one draw needn't show every extreme that they name: `degree_range`: row m holds lo and hi with min(m, 255) <= lo < hi <= 256.
All inputs are finite; a program needn't handle non-finite values.
Results may differ from the reference program's by a relative error of at most 0.0093.
Values may be sent and summed in bfloat16 or wider, within the bound.
No kernel may reach another device: no remote copies, remote signals or barrier semaphores. Data moves between devices by JAX's collectives and lax.ppermute only.
A program may use at most 192 MiB of HBM per device.

```python
import math
import jax
import jax.numpy as jnp
from jax import lax

FRAMES = 256
NLAT = 512
NLON = 1024
DEGREES = 256
ORDERS = 256
OFFSETS = 8


def draw_degree_range(key, part):
    lower_key = jax.random.fold_in(key, 11)
    upper_key = jax.random.fold_in(key, 23)
    orders = jnp.arange(ORDERS, dtype=jnp.int32)
    lower_bits = jax.random.randint(lower_key, (ORDERS,), 0, 1 << 20, dtype=jnp.int32)
    upper_bits = jax.random.randint(upper_key, (ORDERS,), 0, 1 << 20, dtype=jnp.int32)
    largest_width = max(DEGREES // 8, 1)
    lowest = jnp.minimum(orders + lower_bits % largest_width, DEGREES - 1)
    highest = lowest + 1 + upper_bits % (DEGREES - lowest)
    return jnp.stack([lowest, highest], axis=1).astype(jnp.int32)


def plant(entries, own_key, smallest, high):
    dims = entries.shape
    spot = [jax.random.randint(jax.random.fold_in(own_key, axis), (), 0, dims[axis]) for axis in range(len(dims))]
    entries = entries.at[tuple(spot)].set(smallest)
    longest = dims.index(max(dims))
    spot[longest] = (spot[longest] + 1) % dims[longest]
    return entries.at[tuple(spot)].set(high)


def steps_of(key, dims, cuts, low, high):
    level = 1.0
    for dim, parts in cuts:
        draws = jax.random.uniform(jax.random.fold_in(jax.random.fold_in(key, 6), dim), (parts,), jnp.float32, low / len(cuts), high / len(cuts))
        level = level * jnp.repeat(jnp.exp(draws), dims[dim] // parts).reshape((-1,) + (1,) * (len(dims) - 1 - dim))
    return level


def bell_draw(stream_key, dims, width, bound, shards=(), kind=jnp.bfloat16):
    values = jax.random.normal(stream_key, dims, jnp.float32) * width
    if len(shards) > 0:
        values = steps_of(stream_key, dims, shards, -0.22, 0.18) * values
    return jnp.clip(values, min=-bound, max=bound).astype(kind)


def setup_inputs(seed: int = 0) -> dict:
    keys = jax.random.split(jax.random.key(seed), 5)
    return {
        "frames": bell_draw(keys[0], (FRAMES, NLAT, NLON), 1.0, 6.0, ((0, 4), (1, 8))),
        "projection": bell_draw(keys[1], (ORDERS, NLAT, DEGREES), NLAT ** -0.5, 0.25, ((0, 32),)),
        "degree_range": draw_degree_range(jax.random.fold_in(keys[4], 71), 0),
        "offsets": plant(jax.random.randint(keys[3], (OFFSETS,), 0, FRAMES // 4), jax.random.fold_in(keys[3], 1), 0, (FRAMES // 4) - 1).astype(jnp.int32),
    }


def longitude_table(lon_count, order_ids):
    longitude_points = jnp.arange(lon_count, dtype=jnp.int32)
    rotation_radians = longitude_points[:, None] * order_ids[None, :] % lon_count
    angle = rotation_radians.astype(jnp.float32) * (2.0 * math.pi / lon_count)
    factor = 1.0 / math.sqrt(lon_count)
    table = jnp.stack([jnp.cos(angle) * factor, -jnp.sin(angle) * factor], axis=2)
    return table.reshape(lon_count, -1).astype(jnp.bfloat16)

def time_table(entry_total):
    observation_epochs = jnp.arange(entry_total, dtype=jnp.int32)
    rotation_radians = observation_epochs[:, None] * observation_epochs[None, :] % entry_total
    angle = rotation_radians.astype(jnp.float32) * (2.0 * math.pi / entry_total)
    factor = 1.0 / math.sqrt(entry_total)
    cosine = jnp.cos(angle) * factor
    sine = jnp.sin(angle) * factor
    upper = jnp.concatenate([cosine, sine], axis=1)
    lower = jnp.concatenate([-sine, cosine], axis=1)
    return jnp.concatenate([upper, lower], axis=0).astype(jnp.bfloat16)

def reference(frames, projection, degree_range, offsets):
    frame_count, colatitude_total, lon_count = frames.shape
    azimuthal_order_count, _, harmonic_degree_total = projection.shape
    table = longitude_table(lon_count, jnp.arange(azimuthal_order_count, dtype=jnp.int32))
    azimuthal = jnp.dot(frames.reshape(-1, lon_count), table, preferred_element_type=jnp.float32)
    azimuthal = azimuthal.astype(jnp.bfloat16).reshape(frame_count, colatitude_total, azimuthal_order_count, 2)
    by_order = jnp.transpose(azimuthal, (2, 0, 1, 3))
    degrees = jnp.arange(harmonic_degree_total, dtype=jnp.int32)
    keep = ((degrees[None, :] >= degree_range[:, 0:1]) & (degrees[None, :] < degree_range[:, 1:2])).astype(jnp.float32)
    transform = time_table(frame_count)

    def per_order(inputs):
        proj_one, spec_one, keep_one = inputs
        summed = jnp.einsum('tzp,zl->ptl', spec_one.astype(jnp.float32), proj_one.astype(jnp.float32))
        harmonic = (summed * keep_one[None, None, :]).astype(jnp.bfloat16).reshape(2 * frame_count, harmonic_degree_total)
        return jnp.dot(transform, harmonic, preferred_element_type=jnp.float32).astype(jnp.bfloat16)
    spectra = lax.map(per_order, (projection, by_order, keep))
    padded = jnp.concatenate([spectra, jnp.zeros((2, 2 * frame_count, harmonic_degree_total), jnp.bfloat16)], axis=0)
    factor = 1.0 / math.sqrt(frame_count)

    def mode_couple_share(order):
        own = lax.dynamic_index_in_dim(padded, order, 0, keepdims=False).astype(jnp.float32)
        partners = lax.dynamic_slice_in_dim(padded, order + 1, 2, 0).astype(jnp.float32)
        split = partners.reshape(2, 2, frame_count, harmonic_degree_total)
        doubled = jnp.concatenate([split, split], axis=2)
        results = []
        for displacement_position in range(offsets.shape[0]):
            start = (offsets[displacement_position] % frame_count).astype(jnp.int32)
            rolled = lax.dynamic_slice_in_dim(doubled, start, frame_count, 2)
            real_part = rolled.reshape(2, 2 * frame_count, harmonic_degree_total)
            imag_part = jnp.concatenate([rolled[:, 1], -rolled[:, 0]], axis=1)
            both = jnp.concatenate([real_part, imag_part], axis=2)
            results.append(jnp.einsum('rl,srm->slm', own, both))
        stacked = jnp.stack(results, axis=1) * factor
        return stacked.reshape(2, offsets.shape[0], harmonic_degree_total, 2, harmonic_degree_total).astype(jnp.bfloat16)
    return lax.map(mode_couple_share, jnp.arange(azimuthal_order_count, dtype=jnp.int32))
```

```python
import functools
import math

import jax
import jax.numpy as jnp
import numpy as np
from jax import lax
from jax.experimental import pallas as pl
from jax.experimental.pallas import tpu as pltpu
from jax.sharding import PartitionSpec as P

LANES = 128
CHUNK = 2
VMEM_LIMIT = 60 * 1024 * 1024


def shifted(block, axis, distance):
    devices = range(lax.axis_size(axis))
    route = [(i - distance, i) for i in devices if i - distance in devices]
    return lax.ppermute(block, axis, route)


def longitude_rows(lon_count, order_ids):
    phase = np.asarray(order_ids, np.int64)[:, None] * np.arange(lon_count)[None, :] % lon_count
    angle = phase * (2.0 * math.pi / lon_count)
    factor = 1.0 / math.sqrt(lon_count)
    table = np.stack([np.cos(angle) * factor, -np.sin(angle) * factor], axis=1)
    return jnp.asarray(table.reshape(-1, lon_count).astype(np.float32)).astype(jnp.bfloat16)


def azimuthal_kernel(chunks, table_ref, frames_ref, *out_refs):
    groups, steps, lat_rows, lon_count = frames_ref.shape
    first = pl.program_id(0) * steps
    width = groups * lat_rows
    for pair in range(0, steps, 2):
        spans = range(pair, min(pair + 2, steps))
        block = jnp.concatenate(
            [frames_ref[:, g].reshape(width, lon_count) for g in spans], axis=0
        )
        for chunk, out_ref in enumerate(out_refs):
            value = lax.dot_general(
                table_ref[chunk],
                block,
                (((1,), (1,)), ((), ())),
                preferred_element_type=jnp.float32,
            ).astype(jnp.bfloat16)
            for n, g in enumerate(spans):
                part = value[:, n * width : (n + 1) * width]
                out_ref[:, first + g] = part.reshape(part.shape[0] // 2, 2, width)


def azimuthal_transform(table, frames, steps):
    chunks, rows, lon_count = table.shape
    groups, times, lat_rows, _ = frames.shape
    shape = (rows // 2, times, 2, groups * lat_rows)
    return pl.pallas_call(
        functools.partial(azimuthal_kernel, chunks),
        grid=(times // steps,),
        in_specs=[
            pl.BlockSpec((chunks, rows, lon_count), lambda i: (0, 0, 0)),
            pl.BlockSpec((groups, steps, lat_rows, lon_count), lambda i: (0, i, 0, 0)),
        ],
        out_specs=[pl.BlockSpec(shape, lambda i: (0, 0, 0, 0)) for _ in range(chunks)],
        out_shape=[jax.ShapeDtypeStruct(shape, jnp.bfloat16) for _ in range(chunks)],
        compiler_params=pltpu.CompilerParams(vmem_limit_bytes=VMEM_LIMIT),
        cost_estimate=pl.CostEstimate(
            flops=2 * chunks * rows * frames.size,
            bytes_accessed=2 * frames.size,
            transcendentals=0,
        ),
    )(table, frames)


def legendre_kernel(groups, bounds_ref, wire_ref, projection_ref, out_ref, wide):
    _, lat_groups, _, rows, lanes = wire_ref.shape
    degrees = projection_ref.shape[-1]
    lat_rows = lanes // groups
    order = pl.program_id(0)

    @pl.when(order == 0)
    def _():
        wide[...] = jnp.zeros_like(wide)

    for a in range(lat_groups):
        band = projection_ref[0, a * lat_rows : (a + 1) * lat_rows, :]
        for g in range(groups):
            start = a * lanes + g * lat_rows
            wide[start : start + lat_rows, g * degrees : (g + 1) * degrees] = band
    tall = wire_ref.shape[0] * rows
    left = jnp.concatenate(
        [wire_ref[:, a, 0].reshape(tall, lanes) for a in range(lat_groups)], axis=1
    )
    lane = lax.broadcasted_iota(jnp.int32, (tall, degrees), 1)
    keep = (lane >= bounds_ref[order, 0]) & (lane < bounds_ref[order, 1])
    for g in range(groups):
        columns = slice(g * degrees, (g + 1) * degrees)
        summed = jnp.dot(left, wide[:, columns], preferred_element_type=jnp.float32)
        out_ref[0, g * tall : (g + 1) * tall, :] = jnp.where(keep, summed, 0.0).astype(jnp.bfloat16)


def legendre(groups, bounds, wire, projection):
    tm_count, lat_groups, orders, rows, lanes = wire.shape
    _, lat_total, degrees = projection.shape
    total = groups * tm_count * rows
    return pl.pallas_call(
        functools.partial(legendre_kernel, groups),
        grid=(orders,),
        in_specs=[
            pl.BlockSpec(memory_space=pltpu.SMEM),
            pl.BlockSpec((tm_count, lat_groups, 1, rows, lanes), lambda o: (0, 0, o, 0, 0)),
            pl.BlockSpec((1, lat_total, degrees), lambda o: (o, 0, 0)),
        ],
        out_specs=pl.BlockSpec((1, total, degrees), lambda o: (o, 0, 0)),
        out_shape=jax.ShapeDtypeStruct((orders, total, degrees), jnp.bfloat16),
        scratch_shapes=[pltpu.VMEM((lat_groups * lanes, groups * degrees), jnp.bfloat16)],
        compiler_params=pltpu.CompilerParams(vmem_limit_bytes=VMEM_LIMIT),
        cost_estimate=pl.CostEstimate(
            flops=2 * wire.size * groups * degrees,
            bytes_accessed=2 * (wire.size + projection.size),
            transcendentals=0,
        ),
    )(bounds, wire, projection)


def couple_kernel(turn_ref, twice_ref, own_ref, next_ref, *rest):
    out_ref, held, flipped, turned = rest[-4:]
    order, k = pl.program_id(0), pl.program_id(1)
    orders, total, degrees = own_ref.shape
    tall = 2 * degrees

    @pl.when(k == 0)
    def _():
        value = lax.dot_general(
            twice_ref[...],
            own_ref[order],
            (((1,), (1,)), ((), ())),
            preferred_element_type=jnp.float32,
        )
        held[...] = value
        lane = lax.broadcasted_iota(jnp.int32, (tall, total), 1)
        flipped[...] = jnp.where(
            lane % 2 == 0, pltpu.roll(value, total - 1, 1), pltpu.roll(value, 1, 1)
        )

    straight, crossed = turn_ref[k, 0][None], turn_ref[k, 1][None]
    x = held[...].reshape(tall // 8, 8, total)
    y = flipped[...].reshape(tall // 8, 8, total)
    turned[...] = (x * straight + y * crossed).reshape(tall, total).astype(jnp.bfloat16)

    def emit(s, partner):
        product = jnp.dot(turned[...], partner, preferred_element_type=jnp.float32)
        out_ref[0, s, 0] = product.astype(jnp.bfloat16).reshape(degrees, 2, degrees)

    for first in range(orders):

        @pl.when(order == first)
        def _():
            for s in range(2):
                other = first + 1 + s
                emit(s, own_ref[other] if other < orders else next_ref[other - orders])


def couple(turn, twice, own, following, out, first, out_shape):
    offsets = turn.shape[0]
    orders, total, degrees = own.shape
    tall = 2 * degrees
    operands = [turn, twice, own, following]
    specs = [
        pl.BlockSpec(turn.shape, lambda o, k: (0, 0, 0, 0)),
        pl.BlockSpec(twice.shape, lambda o, k: (0, 0)),
        pl.BlockSpec(own.shape, lambda o, k: (0, 0, 0)),
        pl.BlockSpec(following.shape, lambda o, k: (0, 0, 0)),
    ]
    aliases = {}
    if out is not None:
        aliases = {len(operands): 0}
        operands.append(out)
        specs.append(pl.BlockSpec(memory_space=pl.ANY))
    return pl.pallas_call(
        couple_kernel,
        grid=(orders, offsets),
        in_specs=specs,
        out_specs=pl.BlockSpec(
            (1, 2, 1, degrees, 2, degrees), lambda o, k: (o + first, 0, k, 0, 0, 0)
        ),
        out_shape=out_shape,
        scratch_shapes=[
            pltpu.VMEM((tall, total), jnp.float32),
            pltpu.VMEM((tall, total), jnp.float32),
            pltpu.VMEM((tall, total), jnp.bfloat16),
        ],
        input_output_aliases=aliases,
        compiler_params=pltpu.CompilerParams(vmem_limit_bytes=VMEM_LIMIT),
        cost_estimate=pl.CostEstimate(
            flops=4 * orders * offsets * total * tall * degrees,
            bytes_accessed=4 * orders * offsets * tall * degrees,
            transcendentals=0,
        ),
    )(*operands)


def phase_turns(offsets, times, frame_count):
    phase = offsets[:, None] * times[None, :] % frame_count
    angle = phase.astype(jnp.float32) * (2.0 * math.pi / frame_count)
    factor = 1.0 / math.sqrt(frame_count)
    cosine, sine = jnp.cos(angle) * factor, jnp.sin(angle) * factor
    straight = jnp.stack(
        [jnp.stack([cosine, cosine], -1), jnp.stack([-sine, -sine], -1)], axis=1
    )
    crossed = jnp.stack(
        [jnp.stack([-sine, sine], -1), jnp.stack([-cosine, cosine], -1)], axis=1
    )
    turns = jnp.stack([straight, crossed], axis=1)
    turns = turns.reshape(offsets.shape[0], 2, 2, -1)
    return jnp.tile(turns, (1, 1, 4, 1))


def shards(frames, projection, degree_range, offsets):
    frame_rows, lat_rows, lon_count = frames.shape
    orders, lat_total, degrees = projection.shape
    tm_count, lat_groups = lax.axis_size("tm"), lax.axis_size("lat")
    devices = tm_count * lat_groups
    frame_count = frame_rows * tm_count
    groups = LANES // lat_rows
    times = frame_rows // groups
    steps = min(4, times)
    chunks = orders // CHUNK

    ids = np.arange(devices * orders).reshape(devices, chunks, CHUNK)
    table = jnp.stack(
        [longitude_rows(lon_count, ids[:, c].reshape(-1)) for c in range(chunks)], axis=0
    )
    grouped = frames.reshape(groups, times, lat_rows, lon_count)
    sent = list(azimuthal_transform(table[:1], grouped, steps))
    if chunks > 1:
        sent += list(azimuthal_transform(table[1:], grouped, steps))

    rank = lax.axis_index("tm") * lat_groups + lax.axis_index("lat")
    bounds = lax.dynamic_slice_in_dim(degree_range, rank * orders, orders, 0)
    time_ids = (
        np.arange(tm_count)[None, :, None] * frame_rows
        + np.arange(groups)[:, None, None] * times
        + np.arange(times)[None, None, :]
    ).reshape(-1)
    turn = phase_turns(offsets, jnp.asarray(time_ids, jnp.int32), frame_count)
    row = lax.broadcasted_iota(jnp.int32, (2 * degrees, degrees), 0)
    column = lax.broadcasted_iota(jnp.int32, (2 * degrees, degrees), 1)
    twice = (row // 2 == column).astype(jnp.bfloat16)

    harmonics = []
    for c in range(chunks):
        packed = sent[c].reshape(devices, CHUNK * times * 2, LANES)
        moved = lax.all_to_all(packed, ("tm", "lat"), split_axis=0, concat_axis=0, tiled=True)
        wire = moved.reshape(tm_count, lat_groups, CHUNK, times * 2, LANES)
        own = slice(c * CHUNK, (c + 1) * CHUNK)
        harmonics.append(legendre(groups, bounds[own], wire, projection[own]))
    harmonics.append(shifted(harmonics[0], ("tm", "lat"), -1))
    shape = jax.ShapeDtypeStruct(
        (orders, 2, offsets.shape[0], degrees, 2, degrees), jnp.bfloat16
    )
    out = None
    for c in range(chunks):
        out = couple(turn, twice, harmonics[c], harmonics[c + 1], out, c * CHUNK, shape)
    return out


def solution(mesh):
    return jax.shard_map(
        shards,
        mesh=mesh,
        in_specs=(P("tm", "lat", None), P(("tm", "lat"), None, None), P(), P()),
        out_specs=P(("tm", "lat"), None, None, None, None, None),
        check_vma=False,
    )
```

```python
import functools
import math

import jax
import jax.numpy as jnp
import numpy as np
from jax import lax
from jax.experimental import pallas as pl
from jax.experimental.pallas import tpu as pltpu
from jax.sharding import PartitionSpec as P

LANES = 128
VMEM_LIMIT = 60 * 1024 * 1024


def chunk_sizes(orders):
    if orders < 4:
        return [orders]
    return [orders // 2, orders - orders // 2 - 1, 1]


def shifted(block, axis, distance):
    devices = range(lax.axis_size(axis))
    route = [(i - distance, i) for i in devices if i - distance in devices]
    return lax.ppermute(block, axis, route)


def longitude_rows(lon_count, order_ids):
    phase = np.asarray(order_ids, np.int64)[:, None] * np.arange(lon_count)[None, :] % lon_count
    angle = phase * (2.0 * math.pi / lon_count)
    factor = 1.0 / math.sqrt(lon_count)
    table = np.stack([np.cos(angle) * factor, -np.sin(angle) * factor], axis=1)
    return jnp.asarray(table.reshape(-1, lon_count).astype(np.float32)).astype(jnp.bfloat16)


def azimuthal_kernel(steps, count, *refs):
    table_refs, frames_ref, out_refs = refs[:count], refs[count], refs[count + 1 : 2 * count + 1]
    held, stages = refs[2 * count + 1], refs[2 * count + 2 : 3 * count + 2]
    in_sem, out_sem = refs[-2:]
    groups, times, lat_rows, lon_count = frames_ref.shape
    pieces = times // steps
    width = groups * lat_rows

    def load(i):
        span = pl.ds(i * steps, steps)
        return pltpu.make_async_copy(frames_ref.at[:, span], held.at[:, span], in_sem.at[i])

    def save(c, i):
        span = pl.ds(i * steps, steps)
        return pltpu.make_async_copy(
            stages[c].at[:, span], out_refs[c].at[:, span], out_sem.at[c, i]
        )

    for i in range(pieces):
        load(i).start()

    def piece(i, carry):
        load(i).wait()
        for pair in range(0, steps, 2):
            spans = range(pair, min(pair + 2, steps))
            block = jnp.concatenate(
                [held[:, i * steps + g].reshape(width, lon_count) for g in spans], axis=0
            )
            for c in range(count):
                value = lax.dot_general(
                    table_refs[c][...],
                    block,
                    (((1,), (1,)), ((), ())),
                    preferred_element_type=jnp.float32,
                ).astype(jnp.bfloat16)
                for n, g in enumerate(spans):
                    part = value[:, n * width : (n + 1) * width]
                    stages[c][:, i * steps + g] = part.reshape(part.shape[0] // 2, 2, width)
        for c in range(count):
            save(c, i).start()
        return carry

    lax.fori_loop(0, pieces, piece, 0)
    for c in range(count):
        for i in range(pieces):
            save(c, i).wait()


def azimuthal_transform(tables, frames, steps):
    count = len(tables)
    groups, times, lat_rows, _ = frames.shape
    shapes = [(t.shape[0] // 2, times, 2, groups * lat_rows) for t in tables]
    return pl.pallas_call(
        functools.partial(azimuthal_kernel, steps, count),
        in_specs=[pl.BlockSpec(memory_space=pltpu.VMEM)] * count
        + [pl.BlockSpec(memory_space=pl.ANY)],
        out_specs=[pl.BlockSpec(memory_space=pl.ANY)] * count,
        out_shape=[jax.ShapeDtypeStruct(s, jnp.bfloat16) for s in shapes],
        scratch_shapes=[pltpu.VMEM(frames.shape, jnp.bfloat16)]
        + [pltpu.VMEM(s, jnp.bfloat16) for s in shapes]
        + [
            pltpu.SemaphoreType.DMA((times // steps,)),
            pltpu.SemaphoreType.DMA((count, times // steps)),
        ],
        compiler_params=pltpu.CompilerParams(vmem_limit_bytes=VMEM_LIMIT),
        cost_estimate=pl.CostEstimate(
            flops=2 * sum(t.shape[0] for t in tables) * frames.size,
            bytes_accessed=2 * frames.size,
            transcendentals=0,
        ),
    )(*tables, frames)


def legendre_kernel(groups, first, bounds_ref, wire_ref, projection_ref, sort_ref, out_ref, wide):
    _, lat_groups, _, rows, lanes = wire_ref.shape
    degrees = projection_ref.shape[-1]
    lat_rows = lanes // groups
    order = pl.program_id(0)

    @pl.when(order == 0)
    def _():
        wide[...] = jnp.zeros_like(wide)

    for a in range(lat_groups):
        band = projection_ref[0, a * lat_rows : (a + 1) * lat_rows, :]
        for g in range(groups):
            start = a * lanes + g * lat_rows
            wide[start : start + lat_rows, g * degrees : (g + 1) * degrees] = band
    tall = wire_ref.shape[0] * rows
    half = tall // 2
    left = jnp.concatenate(
        [wire_ref[:, a, 0].reshape(tall, lanes) for a in range(lat_groups)], axis=1
    )
    lane = lax.broadcasted_iota(jnp.int32, (tall, degrees), 1)
    low, high = bounds_ref[order + first, 0], bounds_ref[order + first, 1]
    keep = (lane >= low) & (lane < high)
    for g in range(groups):
        columns = slice(g * degrees, (g + 1) * degrees)
        summed = jnp.dot(left, wide[:, columns], preferred_element_type=jnp.float32)
        kept = jnp.where(keep, summed, 0.0).astype(jnp.bfloat16)
        parted = jnp.dot(sort_ref[...], kept, preferred_element_type=jnp.float32)
        parted = parted.astype(jnp.bfloat16)
        for q in range(2):
            start = (q * groups + g) * half
            out_ref[0, start : start + half, :] = parted[q * half : (q + 1) * half, :]


def legendre(groups, first, bounds, wire, projection, sort):
    tm_count, lat_groups, orders, rows, lanes = wire.shape
    _, lat_total, degrees = projection.shape
    total = groups * tm_count * rows
    return pl.pallas_call(
        functools.partial(legendre_kernel, groups, first),
        grid=(orders,),
        in_specs=[
            pl.BlockSpec(memory_space=pltpu.SMEM),
            pl.BlockSpec((tm_count, lat_groups, 1, rows, lanes), lambda o: (0, 0, o, 0, 0)),
            pl.BlockSpec((1, lat_total, degrees), lambda o: (o + first, 0, 0)),
            pl.BlockSpec(sort.shape, lambda o: (0, 0)),
        ],
        out_specs=pl.BlockSpec((1, total, degrees), lambda o: (o, 0, 0)),
        out_shape=jax.ShapeDtypeStruct((orders, total, degrees), jnp.bfloat16),
        scratch_shapes=[pltpu.VMEM((lat_groups * lanes, groups * degrees), jnp.bfloat16)],
        compiler_params=pltpu.CompilerParams(vmem_limit_bytes=VMEM_LIMIT),
        cost_estimate=pl.CostEstimate(
            flops=2 * wire.size * groups * degrees,
            bytes_accessed=2 * wire.size,
            transcendentals=0,
        ),
    )(bounds, wire, projection, sort)


def couple_kernel(jobs, turn_ref, twice_ref, *rest):
    out_ref, own, partner, held, turned_a, turned_b = rest[-6:]
    arrays = rest[:-6]
    job, step = pl.program_id(0), pl.program_id(1)
    total, degrees = own.shape
    half = total // 2
    tall = 2 * degrees
    per_step = out_ref.shape[2]
    last = turn_ref.shape[0] - 1

    def turn(k, target):
        u, v = turn_ref[k, 0][None], turn_ref[k, 1][None]
        x = held[:, :half].reshape(tall // 8, 8, half)
        y = held[:, half:].reshape(tall // 8, 8, half)
        target[:, :half] = (x * u + y * v).reshape(tall, half).astype(jnp.bfloat16)
        target[:, half:] = (y * u - x * v).reshape(tall, half).astype(jnp.bfloat16)

    @pl.when(step == 0)
    def _():
        for n, (mine, other) in enumerate(jobs):

            @pl.when(job == n)
            def _():
                own[...] = arrays[mine[0]][mine[1]]
                partner[...] = arrays[other[0]][other[1]]

        held[...] = lax.dot_general(
            twice_ref[...], own[...], (((1,), (1,)), ((), ())), preferred_element_type=jnp.float32
        )
        turn(0, turned_a)

    pair = lax.broadcasted_iota(jnp.int32, (tall // 8, 8, LANES), 1) % 4 < 2
    for i in range(per_step):
        now, later = (turned_a, turned_b) if i % 2 == 0 else (turned_b, turned_a)
        turn(jnp.minimum(step * per_step + i + 1, last), later)
        product = jnp.dot(now[...], partner[...], preferred_element_type=jnp.float32)
        for n in range(degrees // (2 * LANES)):
            a, b = (
                product[:, (2 * n + t) * LANES : (2 * n + t + 1) * LANES].reshape(
                    tall // 8, 8, LANES
                )
                for t in range(2)
            )
            upper = jnp.where(pair, a, pltpu.roll(b, 2, 1))
            lower = jnp.where(pair, pltpu.roll(a, 6, 1), b)
            mixed = jnp.stack([upper, lower], axis=1).reshape(2 * tall, LANES)
            out_ref[0, 0, i] = mixed.astype(jnp.bfloat16)


def couple(turn, twice, arrays, jobs, places, out, shape):
    offsets, degrees = turn.shape[0], twice.shape[1]
    total = arrays[0].shape[1]
    tall = 2 * degrees
    used = sorted({side[0] for job in jobs for side in job})
    jobs = [tuple((used.index(a), n) for a, n in job) for job in jobs]
    per_step = 2
    operands = [turn, twice] + [arrays[a] for a in used]
    specs = [
        pl.BlockSpec(x.shape, functools.partial(lambda d, *_: (0,) * d, x.ndim)) for x in operands
    ]
    aliases = {}
    kernel = functools.partial(couple_kernel, jobs)
    if out is not None:
        aliases = {len(operands) + 1: 0}
        operands.append(out)
        specs.append(pl.BlockSpec(memory_space=pl.ANY))

    def body(places_ref, *refs):
        kernel(*refs)

    return pl.pallas_call(
        body,
        grid_spec=pltpu.PrefetchScalarGridSpec(
            num_scalar_prefetch=1,
            grid=(len(jobs), offsets // per_step),
            in_specs=specs,
            out_specs=pl.BlockSpec(
                (1, 1, per_step, 2 * tall, LANES),
                lambda j, k, places_ref: (places_ref[2 * j], places_ref[2 * j + 1], k, 0, 0),
            ),
            scratch_shapes=[
                pltpu.VMEM((total, degrees), jnp.bfloat16),
                pltpu.VMEM((total, degrees), jnp.bfloat16),
                pltpu.VMEM((tall, total), jnp.float32),
                pltpu.VMEM((tall, total), jnp.bfloat16),
                pltpu.VMEM((tall, total), jnp.bfloat16),
            ],
        ),
        out_shape=shape,
        input_output_aliases=aliases,
        compiler_params=pltpu.CompilerParams(vmem_limit_bytes=VMEM_LIMIT),
        cost_estimate=pl.CostEstimate(
            flops=2 * len(jobs) * offsets * total * tall * degrees,
            bytes_accessed=2 * len(jobs) * offsets * tall * degrees,
            transcendentals=0,
        ),
    )(jnp.asarray(np.asarray(places, np.int32).reshape(-1)), *operands)


def phase_turns(offsets, times, frame_count):
    phase = offsets[:, None] * times[None, :] % frame_count
    angle = phase.astype(jnp.float32) * (2.0 * math.pi / frame_count)
    factor = 1.0 / math.sqrt(frame_count)
    cosine, sine = jnp.cos(angle) * factor, jnp.sin(angle) * factor
    cosine, sine = cosine[:, None, None, :], sine[:, None, None, :]
    which = jnp.arange(2, dtype=jnp.int32)[None, :, None, None]
    part = jnp.arange(8, dtype=jnp.int32)[None, None, :, None] % 2
    return jnp.where(
        which == 0, jnp.where(part == 0, cosine, -sine), jnp.where(part == 0, -sine, -cosine)
    )


def shards(frames, projection, degree_range, offsets):
    frame_rows, lat_rows, lon_count = frames.shape
    orders, _, degrees = projection.shape
    tm_count, lat_groups = lax.axis_size("tm"), lax.axis_size("lat")
    devices = tm_count * lat_groups
    frame_count = frame_rows * tm_count
    groups = LANES // lat_rows
    times = frame_rows // groups
    steps = min(4, times)
    sizes = chunk_sizes(orders)
    starts = [sum(sizes[:c]) for c in range(len(sizes))]

    ids = np.arange(devices * orders).reshape(devices, orders)
    tables = [
        longitude_rows(lon_count, ids[:, a : a + n].reshape(-1)) for a, n in zip(starts, sizes)
    ]
    grouped = frames.reshape(groups, times, lat_rows, lon_count)
    sent = list(azimuthal_transform(tables[:1], grouped, steps))
    if len(sizes) > 1:
        sent += list(azimuthal_transform(tables[1:], grouped, steps))

    rank = lax.axis_index("tm") * lat_groups + lax.axis_index("lat")
    bounds = lax.dynamic_slice_in_dim(degree_range, rank * orders, orders, 0)
    time_ids = (
        np.arange(tm_count)[None, :, None] * frame_rows
        + np.arange(groups)[:, None, None] * times
        + np.arange(times)[None, None, :]
    ).reshape(-1)
    turn = phase_turns(offsets, jnp.asarray(time_ids, jnp.int32), frame_count)
    row = np.arange(2 * degrees)
    degree_of = row // 8 * 4 + np.array([0, 2, 1, 3])[row % 8 // 2]
    twice = jnp.asarray(degree_of[:, None] == np.arange(degrees)[None, :], jnp.bfloat16)
    tall = tm_count * times * 2
    source = np.arange(tall) % (tall // 2) * 2 + np.arange(tall) // (tall // 2)
    sort = jnp.asarray(source[:, None] == np.arange(tall)[None, :], jnp.bfloat16)

    shape = jax.ShapeDtypeStruct(
        (orders, 2, offsets.shape[0], 2 * degrees * degrees // LANES, LANES), jnp.bfloat16
    )
    spot = [(c, n) for c, size in enumerate(sizes) for n in range(size)]
    spot += [(len(sizes), n) for n in range(2)]
    harmonics = [None] * (len(sizes) + 1)
    done = set()
    out = None
    for c, (start, size) in enumerate(zip(starts, sizes)):
        packed = sent[c].reshape(devices, size * times * 2, LANES)
        moved = lax.all_to_all(packed, ("tm", "lat"), split_axis=0, concat_axis=0, tiled=True)
        wire = moved.reshape(tm_count, lat_groups, size, times * 2, LANES)
        harmonics[c] = legendre(groups, start, bounds, wire, projection, sort)
        if c == 0:
            harmonics[-1] = shifted(harmonics[0][:2], ("tm", "lat"), -1)
        end = start + size
        ready = [
            (o, s)
            for o in range(end)
            for s in range(2)
            if (o, s) not in done
            and (o + 1 + s < end or (o + 1 + s >= orders and (c > 0 or c == len(sizes) - 1)))
        ]
        done.update(ready)
        if ready:
            jobs = [(spot[o], spot[o + 1 + s]) for o, s in ready]
            out = couple(turn, twice, harmonics, jobs, ready, out, shape)
    out = out.reshape(
        orders, 2, offsets.shape[0], degrees, degrees // LANES, 2, LANES
    )
    return jnp.swapaxes(out, 4, 5).reshape(orders, 2, offsets.shape[0], degrees, 2, degrees)


def solution(mesh):
    return jax.shard_map(
        shards,
        mesh=mesh,
        in_specs=(P("tm", "lat", None), P(("tm", "lat"), None, None), P(), P()),
        out_specs=P(("tm", "lat"), None, None, None, None, None),
        check_vma=False,
    )
```

```python
import functools
import math
from typing import NamedTuple

import jax
import jax.numpy as jnp
import numpy as np
from jax import lax
from jax.experimental import pallas as pl
from jax.experimental.pallas import tpu as pltpu
from jax.sharding import PartitionSpec as P

LANES = 128
VMEM_LIMIT = 60 * 1024 * 1024


def chunk_sizes(orders):
    if orders < 6:
        return [orders]
    return [4, 2, 2]


def shifted(block, axis, distance):
    devices = range(lax.axis_size(axis))
    route = [(i - distance, i) for i in devices if i - distance in devices]
    return lax.ppermute(block, axis, route)


def longitude_rows(lon_count, order_ids):
    phase = np.asarray(order_ids, np.int64)[:, None] * np.arange(lon_count)[None, :] % lon_count
    angle = phase * (2.0 * math.pi / lon_count)
    factor = 1.0 / math.sqrt(lon_count)
    table = np.stack([np.cos(angle) * factor, -np.sin(angle) * factor], axis=1)
    return jnp.asarray(table.reshape(-1, lon_count).astype(np.float32)).astype(jnp.bfloat16)


def azimuthal_kernel(steps, count, *refs):
    table_refs, frames_ref, out_refs = refs[:count], refs[count], refs[count + 1 : 2 * count + 1]
    held, stages = refs[2 * count + 1], refs[2 * count + 2 : 3 * count + 2]
    in_sem, out_sem = refs[-2:]
    groups, times, lat_rows, lon_count = frames_ref.shape
    pieces = times // steps
    width = groups * lat_rows

    def load(i):
        span = pl.ds(i * steps, steps)
        return pltpu.make_async_copy(frames_ref.at[:, span], held.at[:, span], in_sem.at[i])

    def save(c, i):
        span = pl.ds(i * steps, steps)
        return pltpu.make_async_copy(
            stages[c].at[:, span], out_refs[c].at[:, span], out_sem.at[c, i]
        )

    for i in range(pieces):
        load(i).start()

    def piece(i, carry):
        load(i).wait()
        for pair in range(0, steps, 2):
            spans = range(pair, min(pair + 2, steps))
            block = jnp.concatenate(
                [held[:, i * steps + g].reshape(width, lon_count) for g in spans], axis=0
            )
            for c in range(count):
                value = lax.dot_general(
                    table_refs[c][...],
                    block,
                    (((1,), (1,)), ((), ())),
                    preferred_element_type=jnp.float32,
                ).astype(jnp.bfloat16)
                for n, g in enumerate(spans):
                    part = value[:, n * width : (n + 1) * width]
                    stages[c][:, i * steps + g] = part.reshape(part.shape[0] // 2, 2, width)
        for c in range(count):
            save(c, i).start()
        return carry

    lax.fori_loop(0, pieces, piece, 0)
    for c in range(count):
        for i in range(pieces):
            save(c, i).wait()


def azimuthal_transform(tables, frames, steps):
    count = len(tables)
    groups, times, lat_rows, _ = frames.shape
    shapes = [(t.shape[0] // 2, times, 2, groups * lat_rows) for t in tables]
    return pl.pallas_call(
        functools.partial(azimuthal_kernel, steps, count),
        in_specs=[pl.BlockSpec(memory_space=pltpu.VMEM)] * count
        + [pl.BlockSpec(memory_space=pl.ANY)],
        out_specs=[pl.BlockSpec(memory_space=pl.ANY)] * count,
        out_shape=[jax.ShapeDtypeStruct(s, jnp.bfloat16) for s in shapes],
        scratch_shapes=[pltpu.VMEM(frames.shape, jnp.bfloat16)]
        + [pltpu.VMEM(s, jnp.bfloat16) for s in shapes]
        + [
            pltpu.SemaphoreType.DMA((times // steps,)),
            pltpu.SemaphoreType.DMA((count, times // steps)),
        ],
        compiler_params=pltpu.CompilerParams(vmem_limit_bytes=VMEM_LIMIT),
        cost_estimate=pl.CostEstimate(
            flops=2 * sum(t.shape[0] for t in tables) * frames.size,
            bytes_accessed=2 * frames.size,
            transcendentals=0,
        ),
    )(*tables, frames)


def joined(ref, *index):
    part = ref.at[index] if index else ref
    return jnp.concatenate([part[n] for n in range(part.shape[0])], axis=1)


def legendre_kernel(groups, first, bounds_ref, wire_ref, projection_ref, sort_ref, twice_ref, *rest):
    harmonic_ref, doubled_ref, wide = rest
    _, lat_groups, _, rows, lanes = wire_ref.shape
    degrees = projection_ref.shape[-1]
    tiles = degrees // LANES
    lat_rows = lanes // groups
    order = pl.program_id(0)

    @pl.when(order == 0)
    def _():
        wide[...] = jnp.zeros_like(wide)

    for a in range(lat_groups):
        band = projection_ref[0, a * lat_rows : (a + 1) * lat_rows, :]
        for g in range(groups):
            start = a * lanes + g * lat_rows
            for n in range(tiles):
                wide[g * tiles + n, start : start + lat_rows] = band[:, n * LANES : (n + 1) * LANES]
    tall = wire_ref.shape[0] * rows
    half = tall // 2
    left = jnp.concatenate(
        [wire_ref[:, a, 0].reshape(tall, lanes) for a in range(lat_groups)], axis=1
    )
    summed = jnp.dot(left, joined(wide), preferred_element_type=jnp.float32)
    lane = lax.broadcasted_iota(jnp.int32, (tall, groups * degrees), 1) % degrees
    low, high = bounds_ref[order + first, 0], bounds_ref[order + first, 1]
    kept = jnp.where((lane >= low) & (lane < high), summed, 0.0).astype(jnp.bfloat16)
    parted = jnp.dot(joined(sort_ref), kept, preferred_element_type=jnp.float32)
    parted = parted.astype(jnp.bfloat16)
    for q in range(2):
        for g in range(groups):
            start = (q * groups + g) * half
            for n in range(tiles):
                column = (g * tiles + n) * LANES
                harmonic_ref[0, n, start : start + half] = parted[
                    q * half : (q + 1) * half, column : column + LANES
                ]
    real, imaginary = (
        jnp.concatenate(
            [
                parted[q * half : (q + 1) * half, g * degrees : (g + 1) * degrees]
                for g in range(groups)
            ],
            axis=0,
        )
        for q in range(2)
    )
    length = groups * half
    for q, pair in enumerate(((real, -imaginary), (imaginary, real))):
        block = lax.dot_general(
            joined(twice_ref),
            jnp.concatenate(pair, axis=1),
            (((1,), (1,)), ((), ())),
            preferred_element_type=jnp.float32,
        ).astype(jnp.bfloat16)
        for n in range(length // LANES):
            doubled_ref[0, q * length // LANES + n] = block[:, n * LANES : (n + 1) * LANES]


def legendre(groups, first, bounds, wire, projection, sort, twice):
    tm_count, lat_groups, orders, rows, lanes = wire.shape
    _, lat_total, degrees = projection.shape
    total = groups * tm_count * rows
    harmonic = (degrees // LANES, total, LANES)
    doubled = (total // LANES, 2 * degrees, LANES)
    return pl.pallas_call(
        functools.partial(legendre_kernel, groups, first),
        grid=(orders,),
        in_specs=[
            pl.BlockSpec(memory_space=pltpu.SMEM),
            pl.BlockSpec((tm_count, lat_groups, 1, rows, lanes), lambda o: (0, 0, o, 0, 0)),
            pl.BlockSpec((1, lat_total, degrees), lambda o: (o + first, 0, 0)),
            pl.BlockSpec(sort.shape, lambda o: (0, 0, 0)),
            pl.BlockSpec(twice.shape, lambda o: (0, 0, 0)),
        ],
        out_specs=[
            pl.BlockSpec((1,) + harmonic, lambda o: (o, 0, 0, 0)),
            pl.BlockSpec((1,) + doubled, lambda o: (o, 0, 0, 0)),
        ],
        out_shape=[
            jax.ShapeDtypeStruct((orders,) + harmonic, jnp.bfloat16),
            jax.ShapeDtypeStruct((orders,) + doubled, jnp.bfloat16),
        ],
        scratch_shapes=[
            pltpu.VMEM((groups * degrees // LANES, lat_groups * lanes, LANES), jnp.bfloat16)
        ],
        compiler_params=pltpu.CompilerParams(vmem_limit_bytes=VMEM_LIMIT),
        cost_estimate=pl.CostEstimate(
            flops=2 * wire.size * groups * degrees,
            bytes_accessed=2 * wire.size,
            transcendentals=0,
        ),
    )(bounds, wire, projection, sort, twice)


def couple_kernel(jobs, own_count, partner_count, plan_ref, turn_ref, *rest):
    owns, partners = rest[:own_count], rest[own_count : own_count + partner_count]
    out_ref, own, raw, partner, turns, turned_a, turned_b, stage, own_sem, raw_sem, out_sem = rest[
        -11:
    ]
    job = pl.program_id(0)
    tiles, total, _ = partner.shape
    degrees = tiles * LANES
    half = total // 2
    tall = 2 * degrees
    offsets = turns.shape[0]

    def fetches(n):
        array, index = jobs[n].partner
        copies = [
            pltpu.make_async_copy(partners[array].at[index], raw.at[n % 2], raw_sem.at[n % 2])
        ]
        for (array, index), buffer in jobs[n].fetched:
            copies.append(
                pltpu.make_async_copy(owns[array].at[index], own.at[buffer], own_sem.at[buffer])
            )
        return copies

    def saves(n):
        return [
            pltpu.make_async_copy(
                stage.at[n % 2, i], out_ref.at[place[0], place[1]], out_sem.at[n % 2, i]
            )
            for i, place in enumerate(jobs[n].places)
        ]

    @pl.when(job == 0)
    def _():
        for copy in fetches(0):
            copy.start()
        for k in range(offsets):
            for n in range(2):
                column = turn_ref[:, 2 * k + n : 2 * k + n + 1]
                turns[k, n] = jnp.broadcast_to(column, (half, LANES))

    for n in range(len(jobs)):

        @pl.when(job == n)
        def _():
            if n + 1 < len(jobs):
                for copy in fetches(n + 1):
                    copy.start()
            for copy in fetches(n):
                copy.wait()
            if n >= 2:
                for copy in saves(n - 2):
                    copy.wait()

    slot = job % 2
    for n in range(tiles):
        partner[n] = raw[slot, n].astype(jnp.float32)

    def turn(k, target):
        cosine, sine = turns[k, 0], turns[k, 1]
        for n in range(tiles):
            x, y = partner[n, :half], partner[n, half:]
            target[n, :half] = (x * cosine + y * sine).astype(jnp.bfloat16)
            target[n, half:] = (y * cosine - x * sine).astype(jnp.bfloat16)

    pair = lax.broadcasted_iota(jnp.int32, (tall // 8, 8, LANES), 1) % 4 < 2

    def products(count):
        turn(0, turned_a)
        for k in range(offsets):
            now, later = (turned_a, turned_b) if k % 2 == 0 else (turned_b, turned_a)
            if k + 1 < offsets:
                turn(k + 1, later)
            for i in range(count):
                left = joined(own, plan_ref[3 * job + 1 + i])
                product = jnp.dot(left, joined(now), preferred_element_type=jnp.float32)
                for n in range(tiles // 2):
                    a, b = (
                        product[:, (2 * n + t) * LANES : (2 * n + t + 1) * LANES].reshape(
                            tall // 8, 8, LANES
                        )
                        for t in range(2)
                    )
                    upper = jnp.where(pair, a, pltpu.roll(b, 2, 1))
                    lower = jnp.where(pair, pltpu.roll(a, 6, 1), b)
                    mixed = jnp.stack([upper, lower], axis=1).reshape(2 * tall, LANES)
                    stage[slot, i, k] = mixed.astype(jnp.bfloat16)

    counts = sorted({len(one.places) for one in jobs})
    for count in counts:
        if len(counts) == 1:
            products(count)
        else:
            pl.when(plan_ref[3 * job] == count)(functools.partial(products, count))

    for n in range(len(jobs)):

        @pl.when(job == n)
        def _():
            for copy in saves(n):
                copy.start()
            if n == len(jobs) - 1:
                for m in range(max(n - 1, 0), n + 1):
                    for copy in saves(m):
                        copy.wait()


class Job(NamedTuple):
    partner: tuple
    fetched: tuple
    buffers: tuple
    places: tuple


def plan_jobs(pairs, spot, own_used, partner_used):
    held, jobs = [None] * 3, []
    for p in sorted({o + 1 + s for o, s in pairs}):
        places = tuple((o, s) for o, s in sorted(pairs, reverse=True) if o + 1 + s == p)
        wanted = [o for o, _ in places]
        busy = [] if not jobs else list(jobs[-1].buffers)
        fetched = []
        for o in wanted:
            if o not in held:
                buffer = next(
                    n for n in range(3) if n not in busy and held[n] not in wanted
                )
                held[buffer] = o
                array, index = spot[o]
                fetched.append(((own_used.index(array), index), buffer))
        array, index = spot[p]
        jobs.append(
            Job(
                (partner_used.index(array), index),
                tuple(fetched),
                tuple(held.index(o) for o in wanted),
                places,
            )
        )
    return jobs


def couple(turn, offsets, doubled, harmonics, pairs, spot, out, shape):
    own_used = sorted({spot[o][0] for o, _ in pairs})
    partner_used = sorted({spot[o + 1 + s][0] for o, s in pairs})
    owns, partners = [doubled[a] for a in own_used], [harmonics[a] for a in partner_used]
    jobs = plan_jobs(pairs, spot, own_used, partner_used)
    _, tiles, total, _ = partners[0].shape
    tall = 2 * tiles * LANES
    plan = [[len(one.places)] + (list(one.buffers) + [0])[:2] for one in jobs]
    operands = [turn] + owns + partners
    specs = [pl.BlockSpec(turn.shape, lambda j, plan_ref: (0, 0))]
    specs += [pl.BlockSpec(memory_space=pl.ANY)] * len(owns + partners)
    aliases = {}
    if out is not None:
        aliases = {len(operands) + 1: 0}
        operands.append(out)
        specs.append(pl.BlockSpec(memory_space=pl.ANY))
    return pl.pallas_call(
        functools.partial(couple_kernel, jobs, len(owns), len(partners)),
        grid_spec=pltpu.PrefetchScalarGridSpec(
            num_scalar_prefetch=1,
            grid=(len(jobs),),
            in_specs=specs,
            out_specs=pl.BlockSpec(memory_space=pl.ANY),
            scratch_shapes=[
                pltpu.VMEM((3,) + owns[0].shape[1:], jnp.bfloat16),
                pltpu.VMEM((2, tiles, total, LANES), jnp.bfloat16),
                pltpu.VMEM((tiles, total, LANES), jnp.float32),
                pltpu.VMEM((offsets, 2, total // 2, LANES), jnp.float32),
                pltpu.VMEM((tiles, total, LANES), jnp.bfloat16),
                pltpu.VMEM((tiles, total, LANES), jnp.bfloat16),
                pltpu.VMEM((2, 2, offsets, 2 * tall, LANES), jnp.bfloat16),
                pltpu.SemaphoreType.DMA((3,)),
                pltpu.SemaphoreType.DMA((2,)),
                pltpu.SemaphoreType.DMA((2, 2)),
            ],
        ),
        out_shape=shape,
        input_output_aliases=aliases,
        compiler_params=pltpu.CompilerParams(vmem_limit_bytes=VMEM_LIMIT),
        cost_estimate=pl.CostEstimate(
            flops=2 * len(pairs) * offsets * total * tall * tiles * LANES,
            bytes_accessed=2 * len(pairs) * offsets * tall * tiles * LANES,
            transcendentals=0,
        ),
    )(jnp.asarray(np.asarray(plan, np.int32).reshape(-1)), *operands)


def tiled_one_hot(columns, width):
    table = np.asarray(columns)[:, None] == np.arange(width)[None, :]
    tiles = table.reshape(len(columns), width // LANES, LANES).swapaxes(0, 1)
    return jnp.asarray(tiles, jnp.bfloat16)


def phase_turns(offsets, times, frame_count):
    lane_offsets = jnp.pad(jnp.repeat(offsets, 2), (0, LANES - 2 * offsets.shape[0]))
    phase = times[:, None] * lane_offsets[None, :] % frame_count
    angle = phase.astype(jnp.float32) * (2.0 * math.pi / frame_count)
    even = jnp.arange(LANES, dtype=jnp.int32)[None, :] % 2 == 0
    return jnp.where(even, jnp.cos(angle), jnp.sin(angle)) * (1.0 / math.sqrt(frame_count))


def shards(frames, projection, degree_range, offsets):
    frame_rows, lat_rows, lon_count = frames.shape
    orders, _, degrees = projection.shape
    tm_count, lat_groups = lax.axis_size("tm"), lax.axis_size("lat")
    devices = tm_count * lat_groups
    frame_count = frame_rows * tm_count
    groups = LANES // lat_rows
    times = frame_rows // groups
    steps = min(8, times)
    sizes = chunk_sizes(orders)
    starts = [sum(sizes[:c]) for c in range(len(sizes))]

    ids = np.arange(devices * orders).reshape(devices, orders)
    tables = [
        longitude_rows(lon_count, ids[:, a : a + n].reshape(-1)) for a, n in zip(starts, sizes)
    ]
    grouped = frames.reshape(groups, times, lat_rows, lon_count)
    sent = list(azimuthal_transform(tables[:1], grouped, steps))
    if len(sizes) > 1:
        sent += list(azimuthal_transform(tables[1:], grouped, steps))

    rank = lax.axis_index("tm") * lat_groups + lax.axis_index("lat")
    bounds = lax.dynamic_slice_in_dim(degree_range, rank * orders, orders, 0)
    time_ids = (
        np.arange(tm_count)[None, :, None] * frame_rows
        + np.arange(groups)[:, None, None] * times
        + np.arange(times)[None, None, :]
    ).reshape(-1)
    turn = phase_turns(offsets, jnp.asarray(time_ids, jnp.int32), frame_count)
    row = np.arange(2 * degrees)
    degree_of = row // 8 * 4 + np.array([0, 2, 1, 3])[row % 8 // 2]
    column_of = degree_of + row % 2 * degrees
    twice = tiled_one_hot(column_of, 2 * degrees)
    tall = tm_count * times * 2
    source = np.arange(tall) % (tall // 2) * 2 + np.arange(tall) // (tall // 2)
    sort = tiled_one_hot(source, tall)

    shape = jax.ShapeDtypeStruct(
        (orders, 2, offsets.shape[0], 2 * degrees * degrees // LANES, LANES), jnp.bfloat16
    )
    spot = [(c, n) for c, size in enumerate(sizes) for n in range(size)]
    spot += [(len(sizes), n) for n in range(2)]
    harmonics = [None] * (len(sizes) + 1)
    doubled = [None] * len(sizes)
    done = set()
    out = None
    for c, (start, size) in enumerate(zip(starts, sizes)):
        packed = sent[c].reshape(devices, size * times * 2, LANES)
        moved = lax.all_to_all(packed, ("tm", "lat"), split_axis=0, concat_axis=0, tiled=True)
        wire = moved.reshape(tm_count, lat_groups, size, times * 2, LANES)
        harmonics[c], doubled[c] = legendre(groups, start, bounds, wire, projection, sort, twice)
        if c == 0:
            harmonics[-1] = shifted(harmonics[0][:2], ("tm", "lat"), -1)
        end = start + size
        ready = [
            (o, s)
            for o in range(end)
            for s in range(2)
            if (o, s) not in done
            and (o + 1 + s < end or (o + 1 + s >= orders and (c > 0 or c == len(sizes) - 1)))
        ]
        done.update(ready)
        if ready:
            out = couple(
                turn, offsets.shape[0], doubled, harmonics, ready, spot, out, shape
            )
    out = out.reshape(
        orders, 2, offsets.shape[0], degrees, degrees // LANES, 2, LANES
    )
    return jnp.swapaxes(out, 4, 5).reshape(orders, 2, offsets.shape[0], degrees, 2, degrees)


def solution(mesh):
    return jax.shard_map(
        shards,
        mesh=mesh,
        in_specs=(P("tm", "lat", None), P(("tm", "lat"), None, None), P(), P()),
        out_specs=P(("tm", "lat"), None, None, None, None, None),
        check_vma=False,
    )
```

```python
import functools
import math
from typing import NamedTuple

import jax
import jax.numpy as jnp
import numpy as np
from jax import lax
from jax.experimental import pallas as pl
from jax.experimental.pallas import tpu as pltpu
from jax.sharding import PartitionSpec as P

LANES = 128
VMEM_LIMIT = 60 * 1024 * 1024


def chunk_sizes(orders):
    if orders < 6:
        return [orders]
    return [orders - 3, 2, 1]


def shifted(block, axis, distance):
    devices = range(lax.axis_size(axis))
    route = [(i - distance, i) for i in devices if i - distance in devices]
    return lax.ppermute(block, axis, route)


def longitude_rows(lon_count, order_ids):
    phase = np.asarray(order_ids, np.int64)[:, None] * np.arange(lon_count)[None, :] % lon_count
    angle = phase * (2.0 * math.pi / lon_count)
    factor = 1.0 / math.sqrt(lon_count)
    table = np.stack([np.cos(angle) * factor, -np.sin(angle) * factor], axis=1)
    return jnp.asarray(table.reshape(-1, lon_count).astype(np.float32)).astype(jnp.bfloat16)


def azimuthal_kernel(steps, count, *refs):
    table_refs, frames_ref, out_refs = refs[:count], refs[count], refs[count + 1 : 2 * count + 1]
    held, stages = refs[2 * count + 1], refs[2 * count + 2 : 3 * count + 2]
    in_sem, out_sem = refs[-2:]
    groups, times, lat_rows, lon_count = frames_ref.shape
    pieces = times // steps
    width = groups * lat_rows

    def load(i):
        span = pl.ds(i * steps, steps)
        return pltpu.make_async_copy(frames_ref.at[:, span], held.at[:, span], in_sem.at[i])

    def save(c, i):
        span = pl.ds(i * steps, steps)
        return pltpu.make_async_copy(
            stages[c].at[:, span], out_refs[c].at[:, span], out_sem.at[c, i]
        )

    for i in range(pieces):
        load(i).start()

    def piece(i, carry):
        load(i).wait()
        for pair in range(0, steps, 2):
            spans = range(pair, min(pair + 2, steps))
            block = jnp.concatenate(
                [held[:, i * steps + g].reshape(width, lon_count) for g in spans], axis=0
            )
            for c in range(count):
                value = lax.dot_general(
                    table_refs[c][...],
                    block,
                    (((1,), (1,)), ((), ())),
                    preferred_element_type=jnp.float32,
                ).astype(jnp.bfloat16)
                for n, g in enumerate(spans):
                    part = value[:, n * width : (n + 1) * width]
                    stages[c][:, i * steps + g] = part.reshape(part.shape[0] // 2, 2, width)
        for c in range(count):
            save(c, i).start()
        return carry

    lax.fori_loop(0, pieces, piece, 0)
    for c in range(count):
        for i in range(pieces):
            save(c, i).wait()


def azimuthal_transform(tables, frames, steps):
    count = len(tables)
    groups, times, lat_rows, _ = frames.shape
    shapes = [(t.shape[0] // 2, times, 2, groups * lat_rows) for t in tables]
    return pl.pallas_call(
        functools.partial(azimuthal_kernel, steps, count),
        in_specs=[pl.BlockSpec(memory_space=pltpu.VMEM)] * count
        + [pl.BlockSpec(memory_space=pl.ANY)],
        out_specs=[pl.BlockSpec(memory_space=pl.ANY)] * count,
        out_shape=[jax.ShapeDtypeStruct(s, jnp.bfloat16) for s in shapes],
        scratch_shapes=[pltpu.VMEM(frames.shape, jnp.bfloat16)]
        + [pltpu.VMEM(s, jnp.bfloat16) for s in shapes]
        + [
            pltpu.SemaphoreType.DMA((times // steps,)),
            pltpu.SemaphoreType.DMA((count, times // steps)),
        ],
        compiler_params=pltpu.CompilerParams(vmem_limit_bytes=VMEM_LIMIT),
        cost_estimate=pl.CostEstimate(
            flops=2 * sum(t.shape[0] for t in tables) * frames.size,
            bytes_accessed=2 * frames.size,
            transcendentals=0,
        ),
    )(*tables, frames)


def joined(ref, *index):
    part = ref.at[index] if index else ref
    return jnp.concatenate([part[n] for n in range(part.shape[0])], axis=1)


def legendre_kernel(groups, first, bounds_ref, wire_ref, projection_ref, sort_ref, twice_ref, *rest):
    harmonic_ref, doubled_ref, wide = rest
    _, lat_groups, _, rows, lanes = wire_ref.shape
    degrees = projection_ref.shape[-1]
    tiles = degrees // LANES
    lat_rows = lanes // groups
    order = pl.program_id(0)

    @pl.when(order == 0)
    def _():
        wide[...] = jnp.zeros_like(wide)

    for a in range(lat_groups):
        band = projection_ref[0, a * lat_rows : (a + 1) * lat_rows, :]
        for g in range(groups):
            start = a * lanes + g * lat_rows
            for n in range(tiles):
                wide[g * tiles + n, start : start + lat_rows] = band[:, n * LANES : (n + 1) * LANES]
    tall = wire_ref.shape[0] * rows
    half = tall // 2
    left = jnp.concatenate(
        [wire_ref[:, a, 0].reshape(tall, lanes) for a in range(lat_groups)], axis=1
    )
    summed = jnp.dot(left, joined(wide), preferred_element_type=jnp.float32)
    lane = lax.broadcasted_iota(jnp.int32, (tall, groups * degrees), 1) % degrees
    low, high = bounds_ref[order + first, 0], bounds_ref[order + first, 1]
    kept = jnp.where((lane >= low) & (lane < high), summed, 0.0).astype(jnp.bfloat16)
    parted = jnp.dot(joined(sort_ref), kept, preferred_element_type=jnp.float32)
    parted = parted.astype(jnp.bfloat16)
    for q in range(2):
        for g in range(groups):
            start = (q * groups + g) * half
            for n in range(tiles):
                column = (g * tiles + n) * LANES
                harmonic_ref[0, n, start : start + half] = parted[
                    q * half : (q + 1) * half, column : column + LANES
                ]
    real, imaginary = (
        jnp.concatenate(
            [
                parted[q * half : (q + 1) * half, g * degrees : (g + 1) * degrees]
                for g in range(groups)
            ],
            axis=0,
        )
        for q in range(2)
    )
    length = groups * half
    for q, pair in enumerate(((real, -imaginary), (imaginary, real))):
        block = lax.dot_general(
            joined(twice_ref),
            jnp.concatenate(pair, axis=1),
            (((1,), (1,)), ((), ())),
            preferred_element_type=jnp.float32,
        ).astype(jnp.bfloat16)
        for n in range(length // LANES):
            doubled_ref[0, q * length // LANES + n] = block[:, n * LANES : (n + 1) * LANES]


def legendre(groups, first, bounds, wire, projection, sort, twice):
    tm_count, lat_groups, orders, rows, lanes = wire.shape
    _, lat_total, degrees = projection.shape
    total = groups * tm_count * rows
    harmonic = (degrees // LANES, total, LANES)
    doubled = (total // LANES, 2 * degrees, LANES)
    return pl.pallas_call(
        functools.partial(legendre_kernel, groups, first),
        grid=(orders,),
        in_specs=[
            pl.BlockSpec(memory_space=pltpu.SMEM),
            pl.BlockSpec((tm_count, lat_groups, 1, rows, lanes), lambda o: (0, 0, o, 0, 0)),
            pl.BlockSpec((1, lat_total, degrees), lambda o: (o + first, 0, 0)),
            pl.BlockSpec(sort.shape, lambda o: (0, 0, 0)),
            pl.BlockSpec(twice.shape, lambda o: (0, 0, 0)),
        ],
        out_specs=[
            pl.BlockSpec((1,) + harmonic, lambda o: (o, 0, 0, 0)),
            pl.BlockSpec((1,) + doubled, lambda o: (o, 0, 0, 0)),
        ],
        out_shape=[
            jax.ShapeDtypeStruct((orders,) + harmonic, jnp.bfloat16),
            jax.ShapeDtypeStruct((orders,) + doubled, jnp.bfloat16),
        ],
        scratch_shapes=[
            pltpu.VMEM((groups * degrees // LANES, lat_groups * lanes, LANES), jnp.bfloat16)
        ],
        compiler_params=pltpu.CompilerParams(vmem_limit_bytes=16 * 1024 * 1024),
        cost_estimate=pl.CostEstimate(
            flops=2 * wire.size * groups * degrees,
            bytes_accessed=2 * wire.size,
            transcendentals=0,
        ),
    )(bounds, wire, projection, sort, twice)


def couple_kernel(jobs, own_count, partner_count, plan_ref, turn_ref, *rest):
    owns, partners = rest[:own_count], rest[own_count : own_count + partner_count]
    out_ref, own, raw, partner, turns, turned_a, turned_b, stage, own_sem, raw_sem, out_sem = rest[
        -11:
    ]
    job = pl.program_id(0)
    tiles, total, _ = partner.shape
    degrees = tiles * LANES
    half = total // 2
    tall = 2 * degrees
    offsets = turns.shape[0]

    def fetches(n):
        array, index = jobs[n].partner
        copies = [
            pltpu.make_async_copy(partners[array].at[index], raw.at[n % 2], raw_sem.at[n % 2])
        ]
        for (array, index), buffer in jobs[n].fetched:
            copies.append(
                pltpu.make_async_copy(owns[array].at[index], own.at[buffer], own_sem.at[buffer])
            )
        return copies

    def saves(n):
        return [
            pltpu.make_async_copy(
                stage.at[n % 2, i], out_ref.at[place[0], place[1]], out_sem.at[n % 2, i]
            )
            for i, place in enumerate(jobs[n].places)
        ]

    @pl.when(job == 0)
    def _():
        for copy in fetches(0):
            copy.start()
        for k in range(offsets):
            for n in range(2):
                column = turn_ref[:, 2 * k + n : 2 * k + n + 1]
                turns[k, n] = jnp.broadcast_to(column, (half, LANES))

    for n in range(len(jobs)):

        @pl.when(job == n)
        def _():
            if n + 1 < len(jobs):
                for copy in fetches(n + 1):
                    copy.start()
            for copy in fetches(n):
                copy.wait()
            if n >= 2:
                for copy in saves(n - 2):
                    copy.wait()

    slot = job % 2
    for n in range(tiles):
        partner[n] = raw[slot, n].astype(jnp.float32)

    def turn(k, target):
        cosine, sine = turns[k, 0], turns[k, 1]
        for n in range(tiles):
            x, y = partner[n, :half], partner[n, half:]
            target[n, :half] = (x * cosine + y * sine).astype(jnp.bfloat16)
            target[n, half:] = (y * cosine - x * sine).astype(jnp.bfloat16)

    pair = lax.broadcasted_iota(jnp.int32, (tall // 8, 8, LANES), 1) % 4 < 2

    def products(count):
        turn(0, turned_a)
        for k in range(offsets):
            now, later = (turned_a, turned_b) if k % 2 == 0 else (turned_b, turned_a)
            if k + 1 < offsets:
                turn(k + 1, later)
            for i in range(count):
                left = joined(own, plan_ref[7 * job + 1 + i])
                product = jnp.dot(left, joined(now), preferred_element_type=jnp.float32)
                for n in range(tiles // 2):
                    a, b = (
                        product[:, (2 * n + t) * LANES : (2 * n + t + 1) * LANES].reshape(
                            tall // 8, 8, LANES
                        )
                        for t in range(2)
                    )
                    upper = jnp.where(pair, a, pltpu.roll(b, 2, 1))
                    lower = jnp.where(pair, pltpu.roll(a, 6, 1), b)
                    mixed = jnp.stack([upper, lower], axis=1).reshape(2 * tall, LANES)
                    stage[slot, i, k] = mixed.astype(jnp.bfloat16)
                pltpu.make_async_copy(
                    stage.at[slot, i, k],
                    out_ref.at[plan_ref[7 * job + 3 + 2 * i], plan_ref[7 * job + 4 + 2 * i], k],
                    out_sem.at[slot, i],
                ).start()

    counts = sorted({len(one.places) for one in jobs})
    for count in counts:
        if len(counts) == 1:
            products(count)
        else:
            pl.when(plan_ref[7 * job] == count)(functools.partial(products, count))

    @pl.when(job == len(jobs) - 1)
    def _():
        for n in range(max(len(jobs) - 2, 0), len(jobs)):
            for copy in saves(n):
                copy.wait()


class Job(NamedTuple):
    partner: tuple
    fetched: tuple
    buffers: tuple
    places: tuple


def plan_jobs(pairs, spot, own_used, partner_used):
    held, jobs = [None] * 3, []
    for p in sorted({o + 1 + s for o, s in pairs}):
        places = tuple((o, s) for o, s in sorted(pairs, reverse=True) if o + 1 + s == p)
        wanted = [o for o, _ in places]
        busy = [] if not jobs else list(jobs[-1].buffers)
        fetched = []
        for o in wanted:
            if o not in held:
                buffer = next(
                    n for n in range(3) if n not in busy and held[n] not in wanted
                )
                held[buffer] = o
                array, index = spot[o]
                fetched.append(((own_used.index(array), index), buffer))
        array, index = spot[p]
        jobs.append(
            Job(
                (partner_used.index(array), index),
                tuple(fetched),
                tuple(held.index(o) for o in wanted),
                places,
            )
        )
    return jobs


def couple(turn, offsets, doubled, harmonics, pairs, spot, out, shape):
    own_used = sorted({spot[o][0] for o, _ in pairs})
    partner_used = sorted({spot[o + 1 + s][0] for o, s in pairs})
    owns, partners = [doubled[a] for a in own_used], [harmonics[a] for a in partner_used]
    jobs = plan_jobs(pairs, spot, own_used, partner_used)
    _, tiles, total, _ = partners[0].shape
    tall = 2 * tiles * LANES
    plan = [
        [len(one.places)]
        + (list(one.buffers) + [0])[:2]
        + (list(sum(one.places, ())) + [0, 0])[:4]
        for one in jobs
    ]
    operands = [turn] + owns + partners
    specs = [pl.BlockSpec(turn.shape, lambda j, plan_ref: (0, 0))]
    specs += [pl.BlockSpec(memory_space=pl.ANY)] * len(owns + partners)
    aliases = {}
    if out is not None:
        aliases = {len(operands) + 1: 0}
        operands.append(out)
        specs.append(pl.BlockSpec(memory_space=pl.ANY))
    return pl.pallas_call(
        functools.partial(couple_kernel, jobs, len(owns), len(partners)),
        grid_spec=pltpu.PrefetchScalarGridSpec(
            num_scalar_prefetch=1,
            grid=(len(jobs),),
            in_specs=specs,
            out_specs=pl.BlockSpec(memory_space=pl.ANY),
            scratch_shapes=[
                pltpu.VMEM((3,) + owns[0].shape[1:], jnp.bfloat16),
                pltpu.VMEM((2, tiles, total, LANES), jnp.bfloat16),
                pltpu.VMEM((tiles, total, LANES), jnp.float32),
                pltpu.VMEM((offsets, 2, total // 2, LANES), jnp.float32),
                pltpu.VMEM((tiles, total, LANES), jnp.bfloat16),
                pltpu.VMEM((tiles, total, LANES), jnp.bfloat16),
                pltpu.VMEM((2, 2, offsets, 2 * tall, LANES), jnp.bfloat16),
                pltpu.SemaphoreType.DMA((3,)),
                pltpu.SemaphoreType.DMA((2,)),
                pltpu.SemaphoreType.DMA((2, 2)),
            ],
        ),
        out_shape=shape,
        input_output_aliases=aliases,
        compiler_params=pltpu.CompilerParams(vmem_limit_bytes=44 * 1024 * 1024),
        cost_estimate=pl.CostEstimate(
            flops=2 * len(pairs) * offsets * total * tall * tiles * LANES,
            bytes_accessed=2 * len(pairs) * offsets * tall * tiles * LANES,
            transcendentals=0,
        ),
    )(jnp.asarray(np.asarray(plan, np.int32).reshape(-1)), *operands)


def tiled_one_hot(columns, width):
    table = np.asarray(columns)[:, None] == np.arange(width)[None, :]
    tiles = table.reshape(len(columns), width // LANES, LANES).swapaxes(0, 1)
    return jnp.asarray(tiles, jnp.bfloat16)


def phase_turns(offsets, times, frame_count):
    lane_offsets = jnp.pad(jnp.repeat(offsets, 2), (0, LANES - 2 * offsets.shape[0]))
    phase = times[:, None] * lane_offsets[None, :] % frame_count
    angle = phase.astype(jnp.float32) * (2.0 * math.pi / frame_count)
    even = jnp.arange(LANES, dtype=jnp.int32)[None, :] % 2 == 0
    return jnp.where(even, jnp.cos(angle), jnp.sin(angle)) * (1.0 / math.sqrt(frame_count))


def shards(frames, projection, degree_range, offsets):
    frame_rows, lat_rows, lon_count = frames.shape
    orders, _, degrees = projection.shape
    tm_count, lat_groups = lax.axis_size("tm"), lax.axis_size("lat")
    devices = tm_count * lat_groups
    frame_count = frame_rows * tm_count
    groups = LANES // lat_rows
    times = frame_rows // groups
    steps = min(8, times)
    sizes = chunk_sizes(orders)
    starts = [sum(sizes[:c]) for c in range(len(sizes))]

    ids = np.arange(devices * orders).reshape(devices, orders)
    tables = [
        longitude_rows(lon_count, ids[:, a : a + n].reshape(-1)) for a, n in zip(starts, sizes)
    ]
    grouped = frames.reshape(groups, times, lat_rows, lon_count)
    sent = list(azimuthal_transform(tables[:1], grouped, steps))
    if len(sizes) > 1:
        sent += list(azimuthal_transform(tables[1:], grouped, min(4, times)))

    rank = lax.axis_index("tm") * lat_groups + lax.axis_index("lat")
    bounds = lax.dynamic_slice_in_dim(degree_range, rank * orders, orders, 0)
    time_ids = (
        np.arange(tm_count)[None, :, None] * frame_rows
        + np.arange(groups)[:, None, None] * times
        + np.arange(times)[None, None, :]
    ).reshape(-1)
    turn = phase_turns(offsets, jnp.asarray(time_ids, jnp.int32), frame_count)
    row = np.arange(2 * degrees)
    degree_of = row // 8 * 4 + np.array([0, 2, 1, 3])[row % 8 // 2]
    column_of = degree_of + row % 2 * degrees
    twice = tiled_one_hot(column_of, 2 * degrees)
    tall = tm_count * times * 2
    source = np.arange(tall) % (tall // 2) * 2 + np.arange(tall) // (tall // 2)
    sort = tiled_one_hot(source, tall)

    shape = jax.ShapeDtypeStruct(
        (orders, 2, offsets.shape[0], 2 * degrees * degrees // LANES, LANES), jnp.bfloat16
    )
    spot = [(c, n) for c, size in enumerate(sizes) for n in range(size)]
    spot += [(len(sizes), n) for n in range(2)]
    harmonics = [None] * (len(sizes) + 1)
    doubled = [None] * len(sizes)
    done = set()
    out = None
    for c, (start, size) in enumerate(zip(starts, sizes)):
        packed = sent[c].reshape(devices, size * times * 2, LANES)
        moved = lax.all_to_all(packed, ("tm", "lat"), split_axis=0, concat_axis=0, tiled=True)
        wire = moved.reshape(tm_count, lat_groups, size, times * 2, LANES)
        harmonics[c], doubled[c] = legendre(groups, start, bounds, wire, projection, sort, twice)
        if c == 0:
            harmonics[-1] = shifted(harmonics[0][:2], ("tm", "lat"), -1)
        end = start + size
        ready = [
            (o, s)
            for o in range(end)
            for s in range(2)
            if (o, s) not in done
            and (o + 1 + s < end or (o + 1 + s >= orders and (c > 0 or c == len(sizes) - 1)))
        ]
        done.update(ready)
        if ready:
            out = couple(
                turn, offsets.shape[0], doubled, harmonics, ready, spot, out, shape
            )
    out = out.reshape(
        orders, 2, offsets.shape[0], degrees, degrees // LANES, 2, LANES
    )
    return jnp.swapaxes(out, 4, 5).reshape(orders, 2, offsets.shape[0], degrees, 2, degrees)


def solution(mesh):
    return jax.shard_map(
        shards,
        mesh=mesh,
        in_specs=(P("tm", "lat", None), P(("tm", "lat"), None, None), P(), P()),
        out_specs=P(("tm", "lat"), None, None, None, None, None),
        check_vma=False,
    )
```
